256 devices in a mesh: slab: 4 (over x), row: 64 (over y, z, core).
Axes of the slice: x: 4, y: 4, z: 8, core: 2. Of those that a mesh axis runs over, the one named last changes fastest.
Arguments:
- forcing: bfloat16 [4, 32768, 64], P('slab', 'row'), may hold values from -6 to 6
- inflow: bfloat16 [32768, 64], P('row'), may hold values from -6 to 6
- self_solve: bfloat16 [4, 64, 512, 512], P('slab', 'row'), may hold values from -0.25 to 0.25
- greens: bfloat16 [4, 64, 20, 512, 512], P('slab', 'row'), may hold values from -0.078125 to 0.078125
- kept_cols: int32 [4, 64, 20], P('slab', 'row'), may hold values from 0 to 63, as said below
- counts: int32 [4, 64], P('slab', 'row'), may hold values from 6 to 20, as said below
Outputs:
- traces: bfloat16 [4, 32768, 64], P('slab', 'row')
The draws below stay inside these ranges and needn't reach their ends.
Inputs may be any that keep to these rules, and one draw needn't show every extreme that they name: `kept_cols`: for each slab and tile row the 20 entries name distinct column tiles. `counts`: in every slab some tile row uses all 20 slots.
All inputs are finite; a program needn't handle non-finite values.
Results may differ from the reference program's by a relative error of at most 0.012.
Values may be sent and summed in bfloat16 or wider, within the bound.
A program may use at most 64 MiB of HBM per device.

```python
import jax
import jax.numpy as jnp
from jax import lax

TILE = 512
N_SLABS = 4
NT = 64
KMAX = 20
NTR = 32768
RHS = 64


def draw_kept_cols(key, part):
    sub = jax.random.fold_in(key, 11)
    scores = jax.random.randint(sub, (N_SLABS, NT, NT), 0, 1 << 20) * NT + jnp.arange(NT, dtype=jnp.int32)
    order = jnp.argsort(scores, axis=-1, stable=True).astype(jnp.int32)
    return order[:, :, :KMAX]


def draw_counts(key, part):
    sub = jax.random.fold_in(key, 23)
    lower = max(1, KMAX // 3)
    values = jax.random.randint(sub, (N_SLABS, NT), lower, KMAX + 1)
    chosen = jax.random.randint(jax.random.fold_in(key, 37), (N_SLABS,), 0, NT)
    places = jnp.arange(NT, dtype=jnp.int32)[None, :]
    return jnp.where(places == chosen[:, None], KMAX, values).astype(jnp.int32)


def shard_levels(own_key, shape, shards, low, high):
    def one(position, shards_of):
        draws = jax.random.uniform(jax.random.fold_in(jax.random.fold_in(own_key, 6), position), (shards_of,), jnp.float32, low / len(shards), high / len(shards))
        return jnp.repeat(jnp.exp(draws), shape[position] // shards_of).reshape((-1,) + (1,) * (len(shape) - position - 1))

    loudness = one(*shards[0])
    for cut in shards[1:]:
        loudness = loudness * one(*cut)
    return loudness


def gaussian(rng, extent, deviation, limit, split=(), held_as=jnp.bfloat16):
    result = jax.random.normal(rng, extent, jnp.float32) * deviation
    if len(split) > 0:
        result = shard_levels(rng, extent, split, -0.22, 0.18) * result
    return jnp.clip(result, min=-limit, max=limit).astype(held_as)


def setup_inputs(seed: int = 0) -> dict:
    key_list = jax.random.split(jax.random.key(seed), 7)
    forcing = gaussian(key_list[0], (N_SLABS, NTR, RHS), 1.0, 6.0, ((0, 4), (1, 64)))
    inflow = gaussian(key_list[1], (NTR, RHS), 1.0, 6.0, ((0, 64),))
    self_solve = gaussian(key_list[2], (N_SLABS, NT, TILE, TILE), TILE ** -0.5, 0.25, ((0, 4), (1, 64)))
    greens = gaussian(key_list[3], (N_SLABS, NT, KMAX, TILE, TILE), (KMAX * TILE // 2 + TILE) ** -0.5, 0.078125, ((0, 4), (1, 64)))
    kept_cols = draw_kept_cols(jax.random.fold_in(key_list[6], 71), 0)
    counts = draw_counts(jax.random.fold_in(key_list[6], 71), 0)
    return {"forcing": forcing, "inflow": inflow, "self_solve": self_solve, "greens": greens, "kept_cols": kept_cols, "counts": counts}


def reference(forcing, inflow, self_solve, greens, kept_cols, counts):
    incoming = inflow
    columns = inflow.shape[1]
    results = []
    slot_ids = jnp.arange(KMAX, dtype=jnp.int32)
    for slab_index in range(N_SLABS):
        tiles = incoming.reshape(NT, TILE, columns)
        sources = forcing[slab_index].reshape(NT, TILE, columns)

        def one_row(items):
            green_row, cols_row, count_row, solve_row, source_row = items
            chosen = tiles[cols_row]
            valid = slot_ids < count_row
            chosen = jnp.where(valid[:, None, None], chosen, jnp.zeros((), chosen.dtype))
            total = jnp.einsum("kij,kjw->iw", green_row.astype(jnp.float32), chosen.astype(jnp.float32))
            coupled = (total + source_row.astype(jnp.float32)).astype(jnp.bfloat16)
            return jnp.dot(solve_row, coupled, preferred_element_type=jnp.float32).astype(jnp.bfloat16)

        outgoing = lax.map(one_row, (greens[slab_index], kept_cols[slab_index], counts[slab_index], self_solve[slab_index], sources))
        outgoing = outgoing.reshape(NT * TILE, columns)
        results.append(outgoing)
        incoming = outgoing
    return jnp.stack(results, axis=0)
```

```python
import functools

import jax
import jax.numpy as jnp
from jax import lax
from jax.experimental import pallas as pl
from jax.experimental.pallas import tpu as pltpu
from jax.sharding import PartitionSpec as P

MESH = pl.DeviceIdType.MESH
NY = 4
CHUNKS = 2
SEGS = 5


def offsets(nz):
    order = [0]
    for d in range(nz // 2, 0, -1):
        order.append(d)
        if d != nz - d:
            order.append(nz - d)
    return order


def nt(a, b):
    return lax.dot_general(a, b, (((1,), (1,)), ((), ())), preferred_element_type=jnp.float32)


def kernel(ns, nz, cols_ref, count_ref, inflow_ref, forcing_ref, solve_hbm, greens_hbm, out_ref,
           *scratch):
    held = scratch[:CHUNKS]
    (sent, greens, solve, acc, local_sem, a_recv, b_recv, r_recv, d_recv, send_sem) = scratch[CHUNKS:]
    chunks, rows = CHUNKS, sent.shape[1]
    kmax = greens.shape[0]
    ny = NY
    s = lax.axis_index("slab")
    r = lax.axis_index("row")
    y, z, c = r // (2 * nz), (r // 2) % nz, r % 2
    up, down = (s + 1) % ns, (s + ns - 1) % ns
    yp, ym, y2 = (y + 1) % ny, (y + ny - 1) % ny, (y + 2) % ny
    order = offsets(nz)

    def at(slab, yy, zz, cc):
        return (slab, yy * (2 * nz) + zz * 2 + cc)

    g_copy = pltpu.make_async_copy(greens_hbm, greens, local_sem.at[0])
    s_copy = pltpu.make_async_copy(solve_hbm, solve, local_sem.at[1])
    g_copy.start()
    s_copy.start()

    barrier = pltpu.get_barrier_semaphore()
    for d in order:
        pl.semaphore_signal(barrier, 1, device_id=at(down, y, (z + d) % nz, c), device_id_type=MESH)
    for peer in (at(s, yp, z, c), at(s, ym, z, c), at(s, y, z, 1 - c)):
        pl.semaphore_signal(barrier, 1, device_id=peer, device_id_type=MESH)
    pl.semaphore_wait(barrier, nz + 3)

    def remote(src, dst, ssem, rsem, peer):
        return pltpu.make_async_remote_copy(
            src_ref=src, dst_ref=dst, send_sem=ssem, recv_sem=rsem, device_id=peer, device_id_type=MESH
        )

    def tile(ch, cc, yy, zz):
        return held[ch].at[cc, yy * nz + zz]

    def group(ch, cc, yy):
        return held[ch].at[cc, pl.ds(yy * nz, nz)]

    def launch(src, ch):
        for p, d in enumerate(order):
            remote(src, tile(ch, c, y, z), send_sem.at[ch, 0], a_recv.at[ch, p],
                   at(up, y, (z + d) % nz, c)).start()

    def step_a(ch, p):
        zz = (z + nz - order[p]) % nz
        t = tile(ch, c, y, zz)
        pltpu.make_async_copy(t, t, a_recv.at[ch, p]).wait()
        remote(t, t, send_sem.at[ch, 1], b_recv.at[ch, 0, p], at(s, yp, z, c)).start()
        remote(t, t, send_sem.at[ch, 1], b_recv.at[ch, 1, p], at(s, ym, z, c)).start()

    def share(ch, yy, i):
        t = group(ch, c, yy)
        remote(t, t, send_sem.at[ch, 3], d_recv.at[ch, i], at(s, y, z, 1 - c)).start()

    def step_b(ch, p):
        zz = (z + nz - order[p]) % nz
        tp, tm = tile(ch, c, ym, zz), tile(ch, c, yp, zz)
        pltpu.make_async_copy(tp, tp, b_recv.at[ch, 0, p]).wait()
        if p % 2 == 0:
            remote(tp, tp, send_sem.at[ch, 2], r_recv.at[ch], at(s, yp, z, c)).start()
        pltpu.make_async_copy(tm, tm, b_recv.at[ch, 1, p]).wait()
        if p % 2 == 1:
            remote(tm, tm, send_sem.at[ch, 2], r_recv.at[ch], at(s, ym, z, c)).start()

    def gather_tail(ch):
        share(ch, y, 0)
        for p in range(nz):
            step_b(ch, p)
        share(ch, ym, 1)
        share(ch, yp, 2)
        g = group(ch, c, y2)
        pltpu.make_async_copy(g, g, r_recv.at[ch]).wait()
        share(ch, y2, 3)
        for i, yy in enumerate((y, ym, yp, y2)):
            g = group(ch, 1 - c, yy)
            pltpu.make_async_copy(g, g, d_recv.at[ch, i]).wait()

    count = count_ref[0]

    def slot(ch, k):
        j = cols_ref[k]
        zlow = jnp.bitwise_and(lax.shift_right_logical(j, 1), nz - 1)
        yhigh = lax.div(j, jnp.int32(2 * nz))
        x = held[ch][jnp.bitwise_and(j, 1), yhigh * nz + zlow]
        x = jnp.where(k < count, x, jnp.zeros_like(x))
        return nt(x, greens[k])

    @pl.when(s == ns - 1)
    def _():
        for ch in range(chunks):
            launch(inflow_ref.at[pl.ds(ch * rows, rows)], ch)

    for p in range(nz):
        step_a(0, p)
    per = kmax // SEGS
    for ch in range(chunks):
        gather_tail(ch)
        if ch == 0:
            g_copy.wait()
            s_copy.wait()
        pending = list(range(nz)) if ch + 1 < chunks else []
        each = -(-nz // (SEGS - 1))
        for seg in range(SEGS):
            total = slot(ch, seg * per)
            for k in range(1, per):
                total += slot(ch, seg * per + k)
            if seg == 0:
                acc[...] = total + forcing_ref[pl.ds(ch * rows, rows)].astype(jnp.float32)
            elif seg < SEGS - 1:
                acc[...] += total
            for p in pending[:each]:
                step_a(ch + 1, p)
            pending = pending[each:]
        coupled = (acc[...] + total).astype(jnp.bfloat16)
        result = nt(coupled, solve[...]).astype(jnp.bfloat16)
        sent[ch] = result
        out_ref[pl.ds(ch * rows, rows)] = result

        @pl.when(s < ns - 1)
        def _():
            launch(sent.at[ch], ch)

    for ch in range(chunks):
        for i, (n, w) in enumerate(((nz, 0), (2 * nz, 0), (nz, 0), (ny * nz, 0))):
            g = held[ch].at[w, pl.ds(0, n)]
            pltpu.make_async_copy(g, g, send_sem.at[ch, i]).wait()


def shards(ns, nrow, forcing, inflow, self_solve, greens, kept_cols, counts):
    nz = nrow // (2 * NY)
    tile, columns = inflow.shape
    kmax = greens.shape[2]
    rows = columns // CHUNKS
    vmem = pl.BlockSpec(memory_space=pltpu.VMEM)
    smem = pl.BlockSpec(memory_space=pltpu.SMEM)
    hbm = pl.BlockSpec(memory_space=pltpu.HBM)
    dma = pltpu.SemaphoreType.DMA
    out = pl.pallas_call(
        functools.partial(kernel, ns, nz),
        name="sweep",
        out_shape=jax.ShapeDtypeStruct((columns, tile), jnp.bfloat16),
        in_specs=[smem, smem, vmem, vmem, hbm, hbm],
        out_specs=vmem,
        scratch_shapes=[
            *[pltpu.VMEM((2, NY * nz, rows, tile), jnp.bfloat16)] * CHUNKS,
            pltpu.VMEM((CHUNKS, rows, tile), jnp.bfloat16),
            pltpu.VMEM((kmax, tile, tile), jnp.bfloat16),
            pltpu.VMEM((tile, tile), jnp.bfloat16),
            pltpu.VMEM((rows, tile), jnp.float32),
            dma((2,)),
            dma((CHUNKS, nz)),
            dma((CHUNKS, 2, nz)),
            dma((CHUNKS,)),
            dma((CHUNKS, 4)),
            dma((CHUNKS, 4)),
        ],
        compiler_params=pltpu.CompilerParams(
            collective_id=0, has_side_effects=True, vmem_limit_bytes=40 * 1024 * 1024
        ),
    )(kept_cols.reshape(kmax), counts.reshape(1), inflow.T, forcing[0].T, self_solve[0, 0], greens[0, 0])
    return out.T[None]


def solution(mesh):
    placed = (
        P("slab", "row", None),
        P("row", None),
        P("slab", "row", None, None),
        P("slab", "row", None, None, None),
        P("slab", "row", None),
        P("slab", "row"),
    )
    return jax.shard_map(
        functools.partial(shards, mesh.shape["slab"], mesh.shape["row"]),
        mesh=mesh, in_specs=placed, out_specs=P("slab", "row", None), check_vma=False,
    )
```

```python
import functools
import jax
import jax.numpy as jnp
from jax import lax
from jax.experimental import pallas as pl
from jax.experimental.pallas import tpu as pltpu
from jax.sharding import PartitionSpec as P

MESH = pl.DeviceIdType.MESH
NY = 4

def offsets(nz):
    order = []
    for d in range(nz // 2, 0, -1):
        order.append(d)
        if d != nz - d:
            order.append(nz - d)
    return order + [0]

def nt(a, b):
    return lax.dot_general(a, b, (((1,), (1,)), ((), ())), preferred_element_type=jnp.float32)

C = 8
F = {'seq': 'AFB', 'lb': 1, 'lf': 2, 'G': 2, 'D': True, 'M': True}


def kernel(ns, nz, cols_ref, count_ref, inflow_hbm, forcing_hbm, solve_hbm, greens_hbm, out_ref, *scratch):
    held = scratch[:C]
    (sent, result, inflow, packed, forcing, greens, turned, solve, solve_t, table, local_sem, g_sem, a_recv, b_recv, d_recv, send_sem) = scratch[C:]
    rows, depth = sent.shape[1:]
    pack = greens.shape[1] // depth
    width = rows // pack
    kmax = greens.shape[0]
    ny = NY
    G = F.get('G', 2)
    s = lax.axis_index("slab")
    r = lax.axis_index("row")
    y, z, c = r // (2 * nz), (r // 2) % nz, r % 2
    up, down = (s + 1) % ns, (s + ns - 1) % ns
    ys = [(y + j) % ny for j in range(ny)]
    order = offsets(nz)
    JS = (2, 1, 3)

    def at(slab, yy, zz, cc):
        return (slab, yy * (2 * nz) + zz * 2 + cc)

    i_copy = pltpu.make_async_copy(inflow_hbm, inflow, local_sem.at[0])
    s_copy = pltpu.make_async_copy(solve_hbm, solve, local_sem.at[1])
    def g_copy(k):
        return pltpu.make_async_copy(greens_hbm.at[k], greens.at[k], g_sem.at[k])
    f_copy = pltpu.make_async_copy(forcing_hbm, forcing, local_sem.at[2])
    i_copy.start()
    f_copy.start()
    s_copy.start()
    for k in range(kmax):
        g_copy(k).start()

    def piece(ref, ch):
        lo = ch * width // rows * rows
        block = ref[pl.ds(lo, rows)].astype(jnp.float32)
        return block[ch * width - lo:ch * width - lo + width]

    def fold(v):
        return jnp.concatenate([v[:, h * depth:(h + 1) * depth] for h in range(pack)], axis=0).astype(jnp.bfloat16)

    barrier = pltpu.get_barrier_semaphore()
    for d in order:
        pl.semaphore_signal(barrier, 1, device_id=at(down, y, (z + d) % nz, c), device_id_type=MESH)
    for j in JS:
        pl.semaphore_signal(barrier, 1, device_id=at(s, ys[j], z, c), device_id_type=MESH)
    pl.semaphore_signal(barrier, 1, device_id=at(s, y, z, 1 - c), device_id_type=MESH)

    for k in range(kmax):
        j = cols_ref[k]
        d = jnp.bitwise_and(z - lax.shift_right_logical(j, 1), nz - 1)
        p = jnp.int32(0)
        for i, o in enumerate(order):
            if i: p = jnp.where(d == o, jnp.int32(i), p)
        table[k] = jnp.bitwise_and(j, 1) * (ny * nz) + lax.div(j, jnp.int32(2 * nz)) * nz + p
    i_copy.wait()
    for ch in range(C):
        packed[ch] = fold(piece(inflow, ch))
    pl.semaphore_wait(barrier, nz + 4)

    def remote(src, dst, ssem, rsem, peer):
        return pltpu.make_async_remote_copy(src_ref=src, dst_ref=dst, send_sem=ssem, recv_sem=rsem, device_id=peer, device_id_type=MESH)

    def block(ch, cc, yy, p, n=1):
        return held[ch].at[pl.ds(cc * (ny * nz) + yy * nz + p, n)]

    def launch(src, ch):
        for p, d in enumerate(order):
            remote(src, block(ch, c, y, p), send_sem.at[ch, 0], a_recv.at[ch, p], at(up, y, (z + d) % nz, c)).start()

    def done(t, sem):
        pltpu.make_async_copy(t, t, sem).wait()

    per_g = nz // G
    def step_a(ch, p):
        t = block(ch, c, y, p)
        done(t, a_recv.at[ch, p])
        for j in JS:
            remote(t, t, send_sem.at[ch, 1], b_recv.at[ch, j - 1, p // per_g], at(s, ys[j], z, c)).start()
        if p % per_g == per_g - 1 and F['D']:
            g = block(ch, c, y, p - per_g + 1, per_g)
            remote(g, g, send_sem.at[ch, 2], d_recv.at[ch, 0, p // per_g], at(s, y, z, 1 - c)).start()

    def step_b(ch, q):
        for j in (1, 3, 2):
            g = block(ch, c, ys[j], q * per_g, per_g)
            done(g, b_recv.at[ch, (ny - j) % ny - 1, q])
            if F['D']:
                remote(g, g, send_sem.at[ch, 2], d_recv.at[ch, j, q], at(s, y, z, 1 - c)).start()

    def finish(ch):
        if F['D']:
            for q in range(G):
                for j in (0, 1, 3, 2):
                    g = block(ch, 1 - c, ys[j], q * per_g, per_g)
                    done(g, d_recv.at[ch, j, q])

    count = count_ref[0]

    def compute(ch):
        totals = [jnp.zeros((rows, turned.shape[2]), jnp.float32)] * pack
        for k in range(kmax):
            x = held[ch][table[k]]
            x = jnp.where(k < count, x, jnp.zeros_like(x))
            for h in range(pack):
                totals[h] += jnp.dot(x, turned[k, pl.ds(h * depth, depth)], preferred_element_type=jnp.float32)
        v = piece(forcing, ch)
        for h in range(pack):
            v += totals[h][h * width:(h + 1) * width]
        v = jnp.dot(v.astype(jnp.bfloat16), solve_t[...], preferred_element_type=jnp.float32)
        sent[ch] = fold(v)

        @pl.when(s < ns - 1)
        def _():
            launch(sent.at[pl.ds(ch, 1)], ch)
        result[pl.ds(ch * width, width)] = v

    @pl.when(s == ns - 1)
    def _():
        for ch in range(C):
            launch(packed.at[pl.ds(ch, 1)], ch)

    def turn(k, carry):
        g_copy(k).wait()
        turned[k] = greens[k].T
        return carry
    lax.fori_loop(0, kmax, turn, 0)
    s_copy.wait()
    solve_t[...] = solve[...].T
    f_copy.wait()

    lb, lf = F['lb'], F['lf']
    for t in range(C + lf):
        for e in F['seq']:
            if e == 'A' and t < C:
                for p in range(nz):
                    step_a(t, p)
            if e == 'B' and 0 <= t - lb < C:
                for q in range(G):
                    step_b(t - lb, q)
            if e == 'F' and 0 <= t - lf < C:
                finish(t - lf)
                compute(t - lf)
    out_ref[...] = result[...].astype(jnp.bfloat16)

    for ch in range(C):
        for i, n in enumerate((nz, 3 * nz, ny * nz)):
            if i == 2 and not F['D']: continue
            g = held[ch].at[pl.ds(0, n)]
            done(g, send_sem.at[ch, i])

def shards(ns, nrow, forcing, inflow, self_solve, greens, kept_cols, counts):
    nz = nrow // (2 * NY)
    tile, columns = inflow.shape
    kmax = greens.shape[2]
    rows = 16
    depth = tile * columns // (C * rows)
    vmem = pl.BlockSpec(memory_space=pltpu.VMEM)
    smem = pl.BlockSpec(memory_space=pltpu.SMEM)
    hbm = pl.BlockSpec(memory_space=pltpu.HBM)
    dma = pltpu.SemaphoreType.DMA
    G = F.get('G', 2)
    out = pl.pallas_call(
        functools.partial(kernel, ns, nz), name="sweep",
        out_shape=jax.ShapeDtypeStruct((columns, tile), jnp.bfloat16),
        in_specs=[smem, smem, hbm, hbm, hbm, hbm], out_specs=vmem,
        scratch_shapes=[
            *[pltpu.VMEM((2 * NY * nz, rows, depth), jnp.bfloat16)] * C,
            pltpu.VMEM((C, rows, depth), jnp.bfloat16),
            pltpu.VMEM((columns, tile), jnp.float32),
            pltpu.VMEM((columns, tile), jnp.bfloat16),
            pltpu.VMEM((C, rows, depth), jnp.bfloat16),
            pltpu.VMEM((columns, tile), jnp.bfloat16),
            pltpu.VMEM((kmax, tile, tile), jnp.bfloat16),
            pltpu.VMEM((kmax, tile, tile), jnp.bfloat16),
            pltpu.VMEM((tile, tile), jnp.bfloat16),
            pltpu.VMEM((tile, tile), jnp.bfloat16),
            pltpu.SMEM((kmax,), jnp.int32),
            dma((3,)), dma((kmax,)), dma((C, nz)), dma((C, 3, G)), dma((C, 4, G)), dma((C, 3)),
        ],
        compiler_params=pltpu.CompilerParams(collective_id=0, has_side_effects=True, vmem_limit_bytes=63 * 1024 * 1024),
    )(kept_cols.reshape(kmax), counts.reshape(1), inflow.T, forcing[0].T, self_solve[0, 0], greens[0, 0])
    return out.T[None]


def solution(mesh):
    placed = (
        P("slab", "row", None),
        P("row", None),
        P("slab", "row", None, None),
        P("slab", "row", None, None, None),
        P("slab", "row", None),
        P("slab", "row"),
    )
    return jax.shard_map(
        functools.partial(shards, mesh.shape["slab"], mesh.shape["row"]),
        mesh=mesh, in_specs=placed, out_specs=P("slab", "row", None), check_vma=False,
    )
```

```python
import functools

import jax
import jax.numpy as jnp
from jax import lax
from jax.experimental import pallas as pl
from jax.experimental.pallas import tpu as pltpu
from jax.sharding import PartitionSpec as P

MESH = pl.DeviceIdType.MESH
NY = 4
ROWS = 16
GROUPS = 1
HOPS = (2, 1, 3)
WIDTHS = (8,) * 8


def offsets(nz):
    order = [0]
    for d in range(1, nz // 2 + 1):
        order.append(d)
        if d != nz - d:
            order.append(nz - d)
    return order


def kernel(widths, ns, nz, cols_ref, count_ref, inflow_hbm, forcing_hbm, solve_hbm, greens_hbm, out_ref, *scratch):
    C = len(widths)
    starts = [sum(widths[:i]) for i in range(C)]
    held, sent, packed = scratch[:C], scratch[C:2 * C], scratch[2 * C:3 * C]
    (inflow, forcing, greens, turned, solve, solve_t, table,
     local_sem, g_sem, a_recv, b_recv, d_recv, send_sem) = scratch[3 * C:]
    tile, kmax, ny = greens.shape[1], greens.shape[0], NY
    s = lax.axis_index("slab")
    r = lax.axis_index("row")
    y, z, c = r // (2 * nz), (r // 2) % nz, r % 2
    ys = [(y + j) % ny for j in range(ny)]
    order = offsets(nz)
    per_g = nz // GROUPS

    def at(slab, yy, zz, cc):
        return (slab, yy * (2 * nz) + zz * 2 + cc)

    own = order.index(0)
    barrier = pltpu.get_barrier_semaphore()

    def greet(*place):
        pl.semaphore_signal(barrier, 1, device_id=at(*place), device_id_type=MESH)

    @pl.when(s == 0)
    def _():
        for d in order:
            if d:
                greet(s, y, (z + d) % nz, c)

    @pl.when(s > 0)
    def _():
        for d in order:
            greet(s - 1, y, (z + d) % nz, c)

    for j in HOPS:
        greet(s, ys[j], z, c)
    greet(s, y, z, 1 - c)

    def g_copy(k):
        return pltpu.make_async_copy(greens_hbm.at[k], greens.at[k], g_sem.at[k])

    i_copy = pltpu.make_async_copy(inflow_hbm, inflow, local_sem.at[0])
    s_copy = pltpu.make_async_copy(solve_hbm, solve, local_sem.at[1])
    f_copy = pltpu.make_async_copy(forcing_hbm, forcing, local_sem.at[2])
    i_copy.start()
    f_copy.start()
    s_copy.start()
    for k in range(kmax):
        g_copy(k).start()

    def piece(ref, ch):
        lo = starts[ch] // ROWS * ROWS
        hi = -(-(starts[ch] + widths[ch]) // ROWS) * ROWS
        block = ref[pl.ds(lo, hi - lo)].astype(jnp.float32)
        return block[starts[ch] - lo:starts[ch] - lo + widths[ch]]

    def fold(v, ch):
        depth = tile * widths[ch] // ROWS
        pieces = [v[:, h * depth:(h + 1) * depth] for h in range(tile // depth)]
        return (jnp.concatenate(pieces, axis=0) if len(pieces) > 1 else v).astype(jnp.bfloat16)

    i_copy.wait()
    for ch in range(C):
        packed[ch][0] = fold(piece(inflow, ch), ch)
    for k in range(kmax):
        j = cols_ref[k]
        d = jnp.bitwise_and(z - lax.shift_right_logical(j, 1), nz - 1)
        p = jnp.int32(0)
        for i, o in enumerate(order):
            p = jnp.where(d == o, jnp.int32(i), p)
        table[k] = jnp.bitwise_and(j, 1) * (ny * nz) + lax.div(j, jnp.int32(2 * nz)) * nz + p

    @pl.when(s == 0)
    def _():
        pl.semaphore_wait(barrier, 2 * nz + 3)

    @pl.when(jnp.logical_and(s > 0, s < ns - 1))
    def _():
        pl.semaphore_wait(barrier, nz + 4)

    @pl.when(s == ns - 1)
    def _():
        pl.semaphore_wait(barrier, 4)

    def remote(src, dst, ssem, rsem, peer):
        return pltpu.make_async_remote_copy(
            src_ref=src, dst_ref=dst, send_sem=ssem, recv_sem=rsem, device_id=peer, device_id_type=MESH
        )

    def done(t, sem):
        pltpu.make_async_copy(t, t, sem).wait()

    def block(ch, cc, yy, p, n=1):
        return held[ch].at[pl.ds(cc * (ny * nz) + yy * nz + p, n)]

    def launch(src, ch):
        for p, d in enumerate(order):
            remote(src, block(ch, c, y, p), send_sem.at[ch, 0], a_recv.at[ch, p], at(s + 1, y, (z + d) % nz, c)).start()

    def share(ch, j, q):
        g = block(ch, c, ys[j], q * per_g, per_g)
        remote(g, g, send_sem.at[ch, 2], d_recv.at[ch, j, q], at(s, y, z, 1 - c)).start()

    def stage_a(ch):
        for p in range(nz):
            t = block(ch, c, y, p)
            if p == own:
                @pl.when(s > 0)
                def _():
                    done(t, a_recv.at[ch, p])
            else:
                done(t, a_recv.at[ch, p])
            for j in HOPS:
                remote(t, t, send_sem.at[ch, 1], b_recv.at[ch, j - 1, p // per_g], at(s, ys[j], z, c)).start()
            if p % per_g == per_g - 1:
                share(ch, 0, p // per_g)

    def stage_b(ch):
        for q in range(GROUPS):
            for j in (1, 3, 2):
                done(block(ch, c, ys[j], q * per_g, per_g), b_recv.at[ch, (ny - j) % ny - 1, q])
                share(ch, j, q)

    count = count_ref[0]

    def arrive(ch):
        for q in range(GROUPS):
            for j in (0, 1, 3, 2):
                done(block(ch, 1 - c, ys[j], q * per_g, per_g), d_recv.at[ch, j, q])

    def finish(ch):
        arrive(ch)
        width, depth = widths[ch], tile * widths[ch] // ROWS
        pack = tile // depth
        totals = [jnp.zeros((ROWS, tile), jnp.float32)] * pack
        for k in range(kmax):
            x = held[ch][table[k]]
            x = jnp.where(k < count, x, jnp.zeros_like(x))
            for h in range(pack):
                totals[h] += jnp.dot(x, turned[k, pl.ds(h * depth, depth)], preferred_element_type=jnp.float32)
        v = piece(forcing, ch)
        for h in range(pack):
            v += totals[h][h * width:(h + 1) * width]
        v = jnp.dot(v.astype(jnp.bfloat16), solve_t[...], preferred_element_type=jnp.float32)
        sent[ch][0] = fold(v, ch)

        @pl.when(s < ns - 1)
        def _():
            launch(sent[ch], ch)
        out_ref[pl.ds(starts[ch], width)] = v

    @pl.when(s == 0)
    def _():
        for ch in range(C):
            for p, d in enumerate(order):
                if d:
                    remote(packed[ch], block(ch, c, y, p), send_sem.at[ch, 3], a_recv.at[ch, p],
                           at(s, y, (z + d) % nz, c)).start()
            held[ch][pl.ds(c * (ny * nz) + y * nz + own, 1)] = packed[ch][...]

    def turn(k, carry):
        g_copy(k).wait()
        turned[k] = greens[k].T
        return carry

    lax.fori_loop(0, kmax, turn, 0)
    s_copy.wait()
    solve_t[...] = solve[...].T
    f_copy.wait()

    for t in range(C + 2):
        if t < C:
            stage_a(t)
        if t >= 2:
            finish(t - 2)
        if 1 <= t <= C:
            stage_b(t - 1)

    def left(i, n):
        for ch in range(C):
            done(held[ch].at[pl.ds(0, n)], send_sem.at[ch, i])

    @pl.when(s == 0)
    def _():
        left(3, nz - 1)

    @pl.when(s < ns - 1)
    def _():
        left(0, nz)

    left(1, 3 * nz)
    left(2, ny * nz)


def shards(widths, ns, nrow, forcing, inflow, self_solve, greens, kept_cols, counts, name="sweep"):
    nz = nrow // (2 * NY)
    tile, columns = inflow.shape
    kmax = greens.shape[2]
    C = len(widths)
    smem = pl.BlockSpec(memory_space=pltpu.SMEM)
    hbm = pl.BlockSpec(memory_space=pltpu.HBM)
    dma = pltpu.SemaphoreType.DMA
    bf16 = jnp.bfloat16

    def chunk(n, w):
        return pltpu.VMEM((n, ROWS, tile * w // ROWS), bf16)

    out = pl.pallas_call(
        functools.partial(kernel, widths, ns, nz),
        name=name,
        out_shape=jax.ShapeDtypeStruct((columns, tile), jnp.float32),
        in_specs=[smem, smem, hbm, hbm, hbm, hbm],
        out_specs=pl.BlockSpec(memory_space=pltpu.VMEM),
        scratch_shapes=[
            *[chunk(2 * NY * nz, w) for w in widths],
            *[chunk(1, w) for w in widths],
            *[chunk(1, w) for w in widths],
            pltpu.VMEM((columns, tile), bf16),
            pltpu.VMEM((columns, tile), bf16),
            pltpu.VMEM((kmax, tile, tile), bf16),
            pltpu.VMEM((kmax, tile, tile), bf16),
            pltpu.VMEM((tile, tile), bf16),
            pltpu.VMEM((tile, tile), bf16),
            pltpu.SMEM((kmax,), jnp.int32),
            dma((3,)),
            dma((kmax,)),
            dma((C, nz)),
            dma((C, NY - 1, GROUPS)),
            dma((C, NY, GROUPS)),
            dma((C, 4)),
        ],
        compiler_params=pltpu.CompilerParams(
            collective_id=0, has_side_effects=True, vmem_limit_bytes=63 * 1024 * 1024
        ),
    )(kept_cols.reshape(kmax), counts.reshape(1), inflow.T, forcing[0].T, self_solve[0, 0], greens[0, 0])
    return out.astype(bf16).T[None]


def solution(mesh):
    placed = (
        P("slab", "row", None),
        P("row", None),
        P("slab", "row", None, None),
        P("slab", "row", None, None, None),
        P("slab", "row", None),
        P("slab", "row"),
    )
    return jax.shard_map(
        functools.partial(shards, WIDTHS, mesh.shape["slab"], mesh.shape["row"]),
        mesh=mesh, in_specs=placed, out_specs=P("slab", "row", None), check_vma=False,
    )
```

```python
import functools

import jax
import jax.numpy as jnp
from jax import lax
from jax.experimental import pallas as pl
from jax.experimental.pallas import tpu as pltpu
from jax.sharding import PartitionSpec as P

MESH = pl.DeviceIdType.MESH
NY = 4
ROWS = 16
GROUPS = 1
HOPS = (2, 1, 3)
WIDTHS = (8,) * 8


def offsets(nz):
    order = [0]
    for d in range(1, nz // 2 + 1):
        order.append(d)
        if d != nz - d:
            order.append(nz - d)
    return order


def kernel(widths, ns, nz, cols_ref, count_ref, inflow_hbm, forcing_hbm, solve_hbm, greens_hbm, out_ref, *scratch):
    C = len(widths)
    starts = [sum(widths[:i]) for i in range(C)]
    held, sent, packed = scratch[:C], scratch[C:2 * C], scratch[2 * C:3 * C]
    (inflow, forcing, greens, turned, solve, solve_t, table,
     local_sem, g_sem, a_recv, b_recv, d_recv, send_sem) = scratch[3 * C:]
    tile, kmax, ny = greens.shape[1], greens.shape[0], NY
    s = lax.axis_index("slab")
    r = lax.axis_index("row")
    y, z, c = r // (2 * nz), (r // 2) % nz, r % 2
    ys = [(y + j) % ny for j in range(ny)]
    order = offsets(nz)
    per_g = nz // GROUPS

    def at(slab, yy, zz, cc):
        return (slab, yy * (2 * nz) + zz * 2 + cc)

    own = order.index(0)
    barrier = pltpu.get_barrier_semaphore()

    def greet(*place):
        pl.semaphore_signal(barrier, 1, device_id=at(*place), device_id_type=MESH)

    @pl.when(s == 0)
    def _():
        for d in order:
            if d:
                greet(s, y, (z + d) % nz, c)

    @pl.when(s > 0)
    def _():
        for d in order:
            greet(s - 1, y, (z + d) % nz, c)

    for j in HOPS:
        greet(s, ys[j], z, c)
    greet(s, y, z, 1 - c)

    def g_copy(k):
        return pltpu.make_async_copy(greens_hbm.at[k], greens.at[k], g_sem.at[k])

    i_copy = pltpu.make_async_copy(inflow_hbm, inflow, local_sem.at[0])
    s_copy = pltpu.make_async_copy(solve_hbm, solve, local_sem.at[1])
    f_copy = pltpu.make_async_copy(forcing_hbm, forcing, local_sem.at[2])
    i_copy.start()
    f_copy.start()
    s_copy.start()
    for k in range(kmax):
        g_copy(k).start()

    def piece(ref, ch):
        lo = starts[ch] // ROWS * ROWS
        hi = -(-(starts[ch] + widths[ch]) // ROWS) * ROWS
        block = ref[pl.ds(lo, hi - lo)].astype(jnp.float32)
        return block[starts[ch] - lo:starts[ch] - lo + widths[ch]]

    def fold(v, ch):
        depth = tile * widths[ch] // ROWS
        pieces = [v[:, h * depth:(h + 1) * depth] for h in range(tile // depth)]
        return (jnp.concatenate(pieces, axis=0) if len(pieces) > 1 else v).astype(jnp.bfloat16)

    i_copy.wait()
    for ch in range(C):
        packed[ch][0] = fold(piece(inflow, ch), ch)
    for k in range(kmax):
        j = cols_ref[k]
        d = jnp.bitwise_and(z - lax.shift_right_logical(j, 1), nz - 1)
        p = jnp.int32(0)
        for i, o in enumerate(order):
            p = jnp.where(d == o, jnp.int32(i), p)
        table[k] = jnp.bitwise_and(j, 1) * (ny * nz) + lax.div(j, jnp.int32(2 * nz)) * nz + p

    @pl.when(s == 0)
    def _():
        pl.semaphore_wait(barrier, 2 * nz + 3)

    @pl.when(jnp.logical_and(s > 0, s < ns - 1))
    def _():
        pl.semaphore_wait(barrier, nz + 4)

    @pl.when(s == ns - 1)
    def _():
        pl.semaphore_wait(barrier, 4)

    def remote(src, dst, ssem, rsem, peer):
        return pltpu.make_async_remote_copy(
            src_ref=src, dst_ref=dst, send_sem=ssem, recv_sem=rsem, device_id=peer, device_id_type=MESH
        )

    def done(t, sem):
        pltpu.make_async_copy(t, t, sem).wait()

    def block(ch, cc, yy, p, n=1):
        return held[ch].at[pl.ds(cc * (ny * nz) + yy * nz + p, n)]

    def launch(src, ch):
        for p, d in enumerate(order):
            remote(src, block(ch, c, y, p), send_sem.at[ch, 0], a_recv.at[ch, p], at(s + 1, y, (z + d) % nz, c)).start()

    def share(ch, j, q):
        g = block(ch, c, ys[j], q * per_g, per_g)
        remote(g, g, send_sem.at[ch, 2], d_recv.at[ch, j, q], at(s, y, z, 1 - c)).start()

    def stage_a(ch):
        for p in range(nz):
            t = block(ch, c, y, p)
            if p == own:
                @pl.when(s > 0)
                def _():
                    done(t, a_recv.at[ch, p])
            else:
                done(t, a_recv.at[ch, p])
            for j in HOPS:
                remote(t, t, send_sem.at[ch, 1], b_recv.at[ch, j - 1, p // per_g], at(s, ys[j], z, c)).start()
            if p % per_g == per_g - 1:
                share(ch, 0, p // per_g)

    def stage_b(ch):
        for q in range(GROUPS):
            for j in (1, 3, 2):
                done(block(ch, c, ys[j], q * per_g, per_g), b_recv.at[ch, (ny - j) % ny - 1, q])
                share(ch, j, q)

    count = count_ref[0]

    def arrive(ch):
        for q in range(GROUPS):
            for j in (0, 1, 3, 2):
                done(block(ch, 1 - c, ys[j], q * per_g, per_g), d_recv.at[ch, j, q])

    def finish(ch):
        arrive(ch)
        width, depth = widths[ch], tile * widths[ch] // ROWS
        pack = tile // depth
        totals = [jnp.zeros((ROWS, tile), jnp.float32)] * pack
        for k in range(kmax):
            x = held[ch][table[k]]
            x = jnp.where(k < count, x, jnp.zeros_like(x))
            for h in range(pack):
                totals[h] += jnp.dot(x, turned[k, pl.ds(h * depth, depth)], preferred_element_type=jnp.float32)
        v = piece(forcing, ch)
        for h in range(pack):
            v += totals[h][h * width:(h + 1) * width]
        v = jnp.dot(v.astype(jnp.bfloat16), solve_t[...], preferred_element_type=jnp.float32)
        sent[ch][0] = fold(v, ch)

        @pl.when(s < ns - 1)
        def _():
            launch(sent[ch], ch)
        out_ref[pl.ds(starts[ch], width)] = v

    @pl.when(s == 0)
    def _():
        for ch in range(C):
            for p, d in enumerate(order):
                if d:
                    remote(packed[ch], block(ch, c, y, p), send_sem.at[ch, 3], a_recv.at[ch, p],
                           at(s, y, (z + d) % nz, c)).start()
            held[ch][pl.ds(c * (ny * nz) + y * nz + own, 1)] = packed[ch][...]

    def turn(k, carry):
        g_copy(k).wait()
        turned[k] = greens[k].T
        return carry

    lax.fori_loop(0, kmax, turn, 0)
    s_copy.wait()
    solve_t[...] = solve[...].T
    f_copy.wait()

    for t in range(C + 2):
        if t < C:
            stage_a(t)
        if t >= 2:
            finish(t - 2)
        if 1 <= t <= C:
            stage_b(t - 1)

    def left(i, n):
        for ch in range(C):
            done(held[ch].at[pl.ds(0, n)], send_sem.at[ch, i])

    @pl.when(s == 0)
    def _():
        left(3, nz - 1)

    @pl.when(s < ns - 1)
    def _():
        left(0, nz)

    left(1, 3 * nz)
    left(2, ny * nz)


def shards(widths, ns, nrow, forcing, inflow, self_solve, greens, kept_cols, counts, name="sweep"):
    nz = nrow // (2 * NY)
    tile, columns = inflow.shape
    kmax = greens.shape[2]
    C = len(widths)
    smem = pl.BlockSpec(memory_space=pltpu.SMEM)
    hbm = pl.BlockSpec(memory_space=pltpu.HBM)
    dma = pltpu.SemaphoreType.DMA
    bf16 = jnp.bfloat16

    def pin(v):
        return pltpu.with_memory_space_constraint(v, pltpu.HBM)

    def chunk(n, w):
        return pltpu.VMEM((n, ROWS, tile * w // ROWS), bf16)

    out = pl.pallas_call(
        functools.partial(kernel, widths, ns, nz),
        name=name,
        out_shape=jax.ShapeDtypeStruct((columns, tile), jnp.float32),
        in_specs=[smem, smem, hbm, hbm, hbm, hbm],
        out_specs=pl.BlockSpec(memory_space=pltpu.VMEM),
        scratch_shapes=[
            *[chunk(2 * NY * nz, w) for w in widths],
            *[chunk(1, w) for w in widths],
            *[chunk(1, w) for w in widths],
            pltpu.VMEM((columns, tile), bf16),
            pltpu.VMEM((columns, tile), bf16),
            pltpu.VMEM((kmax, tile, tile), bf16),
            pltpu.VMEM((kmax, tile, tile), bf16),
            pltpu.VMEM((tile, tile), bf16),
            pltpu.VMEM((tile, tile), bf16),
            pltpu.SMEM((kmax,), jnp.int32),
            dma((3,)),
            dma((kmax,)),
            dma((C, nz)),
            dma((C, NY - 1, GROUPS)),
            dma((C, NY, GROUPS)),
            dma((C, 4)),
        ],
        compiler_params=pltpu.CompilerParams(
            collective_id=0, has_side_effects=True, vmem_limit_bytes=40 * 1024 * 1024,
        ),
    )(pin(kept_cols.reshape(kmax)), counts.reshape(1), pin(inflow.T), pin(forcing[0].T), pin(self_solve[0, 0]), pin(greens[0, 0]))
    return out.astype(bf16).T[None]


def solution(mesh):
    placed = (
        P("slab", "row", None),
        P("row", None),
        P("slab", "row", None, None),
        P("slab", "row", None, None, None),
        P("slab", "row", None),
        P("slab", "row"),
    )
    return jax.shard_map(
        functools.partial(shards, WIDTHS, mesh.shape["slab"], mesh.shape["row"]),
        mesh=mesh, in_specs=placed, out_specs=P("slab", "row", None), check_vma=False,
    )
```
